256 devices in a mesh: row: 8 (over z_lo, core), col: 32 (over z_hi, y, x).
Axes of the slice: x: 4, y: 4, z: 8 (z_hi: 2, z_lo: 4; z = z_hi * 4 + z_lo), core: 2. Of those that a mesh axis runs over, the one named last changes fastest.
Arguments:
- features: bfloat16 [512, 768], P(('row', 'col')), may hold values from -6 to 13
- projection: bfloat16 [768, 768], replicated, may hold values from -1 to 2
- classifiers: bfloat16 [786432, 768], P(('row', 'col')), may hold values from -2 to 1
- positive_ids: int32 [512, 8], P(('row', 'col')), may hold values from 0 to 786431, as said below
Outputs:
- new_classifiers: bfloat16 [786432, 768], P(('row', 'col'))
- projection_grad: bfloat16 [768, 768], replicated
- features_grad: bfloat16 [512, 768], P(('row', 'col'))
The draws below stay inside these ranges and needn't reach their ends.
Inputs may be any that keep to these rules, and one draw needn't show every extreme that they name: `positive_ids`: the k-th id of every row lies in [k * 98304, (k + 1) * 98304).
All inputs are finite; a program needn't handle non-finite values.
Results may differ from the reference program's by a relative error of at most 0.0012.
The reference program's roundings to bfloat16 on the way (of `emb`, `score_grad` and `emb_grad`) count: a program that leaves them out, or rounds other values in their place, can miss the bound.
Values may be sent and summed in bfloat16 or wider, within the bound.
No kernel may reach another device: no remote copies, remote signals or barrier semaphores. Data moves between devices by JAX's collectives and lax.ppermute only.
A program may use at most 192 MiB of HBM per device.

```python
import jax
import jax.numpy as jnp
from jax import lax

D = 768
LAB_DEV = 3072
POSITIVES = 8
BATCH = 512
LABELS = 786432


def draw_positive_ids(key, part):
    segment = LABELS // POSITIVES
    offsets = jax.random.randint(key, (BATCH, POSITIVES), 0, segment)
    return (offsets + jnp.arange(POSITIVES, dtype=jnp.int32)[None, :] * segment).astype(jnp.int32)


def leading_level():
    level = jnp.log(jnp.float32(LABELS))
    return level - jnp.log(level) + 0.5


def draw_features(key, part):
    first = jax.random.fold_in(key, 101)
    second = jax.random.fold_in(key, 102)
    others = jnp.clip(jax.random.normal(first, (BATCH, D), jnp.float32), -6.0, 6.0)
    leading = leading_level() * jax.random.uniform(second, (BATCH, 1), jnp.float32, 0.93, 1.07)
    return jnp.concatenate([leading, others[:, 1:]], axis=1).astype(jnp.bfloat16)


def draw_projection(key, part):
    first = jax.random.fold_in(key, 201)
    second = jax.random.fold_in(key, 202)
    scale = 1.0 / jnp.sqrt(jnp.float32(D))
    matrix = jnp.clip(jax.random.normal(first, (D, D), jnp.float32), -6.0, 6.0) * scale
    corner = jax.random.uniform(second, (), jnp.float32, 0.97, 1.03)
    return matrix.at[0, 0].set(corner).astype(jnp.bfloat16)


def draw_classifiers(key, part):
    first = jax.random.fold_in(key, 301)
    second = jax.random.fold_in(key, 302)
    scale = 1.0 / jnp.sqrt(jnp.float32(D))
    others = jnp.clip(jax.random.normal(first, (LABELS, D), jnp.float32), -6.0, 6.0) * scale
    leading = -jax.random.uniform(second, (LABELS, 1), jnp.float32, 1.0, 1.6)
    return jnp.concatenate([leading, others[:, 1:]], axis=1).astype(jnp.bfloat16)


def setup_inputs(seed: int = 0) -> dict:
    key_of = jax.random.split(jax.random.key(seed), 5)
    features = draw_features(jax.random.fold_in(key_of[4], 71), 0)
    projection = draw_projection(jax.random.fold_in(key_of[4], 71), 0)
    classifiers = draw_classifiers(jax.random.fold_in(key_of[4], 71), 0)
    positive_ids = draw_positive_ids(jax.random.fold_in(key_of[4], 71), 0)
    return {"features": features, "projection": projection, "classifiers": classifiers, "positive_ids": positive_ids}


learn_rate = 1.0


def reference(features, projection, classifiers, positive_ids):
    emb = jnp.dot(features, projection, preferred_element_type=jnp.float32).astype(jnp.bfloat16)
    blocks = classifiers.reshape(LABELS // LAB_DEV, LAB_DEV, D)

    def one_block(carry, inputs):
        weights, index = inputs
        logits = lax.dot_general(emb, weights, (((1,), (1,)), ((), ())), preferred_element_type=jnp.float32)
        label_ids = index * LAB_DEV + jnp.arange(LAB_DEV, dtype=jnp.int32)
        target = jnp.zeros(logits.shape, jnp.float32)
        for k in range(POSITIVES):
            target = target + (positive_ids[:, k][:, None] == label_ids[None, :]).astype(jnp.float32)
        score_grad = ((jax.nn.sigmoid(logits) - target) / BATCH).astype(jnp.bfloat16)
        carry = carry + jnp.dot(score_grad, weights, preferred_element_type=jnp.float32)
        update = lax.dot_general(score_grad, emb, (((0,), (0,)), ((), ())), preferred_element_type=jnp.float32)
        fresh = (weights.astype(jnp.float32) - learn_rate * update).astype(jnp.bfloat16)
        return carry, fresh

    indices = jnp.arange(LABELS // LAB_DEV, dtype=jnp.int32)
    summed, fresh = lax.scan(one_block, jnp.zeros((BATCH, D), jnp.float32), (blocks, indices))
    emb_grad = summed.astype(jnp.bfloat16)
    projection_grad = lax.dot_general(features, emb_grad, (((0,), (0,)), ((), ())), preferred_element_type=jnp.float32).astype(jnp.bfloat16)
    features_grad = lax.dot_general(emb_grad, projection, (((1,), (1,)), ((), ())), preferred_element_type=jnp.float32).astype(jnp.bfloat16)
    return fresh.reshape(LABELS, D), projection_grad, features_grad
```

```python
import jax
import jax.numpy as jnp
from jax import lax
from jax.experimental import pallas as pl
from jax.experimental.pallas import tpu as pltpu
from jax.sharding import Mesh
from jax.sharding import PartitionSpec as P

AXES = ("zl", "core", "zh", "y", "x")
PLANE = ("y", "x")
LINE = ("zh", "zl")
CHIPS = PLANE + LINE
CORE = "core"
SWAP = ((0, 1), (1, 0))
LANES = 128
SHIFTS = (12, 6, 0)
LABEL_TILE = 768

learn_rate = 1.0
bf16 = jnp.bfloat16
f32 = jnp.float32


def copies_to(sent, axes):
    return lax.all_to_all(sent, axes, 0, 0, tiled=True)


def matmul(a, b, over):
    return lax.dot_general(a, b, (over, ((), ())), preferred_element_type=f32)


def whole(shape, buffers=None):
    mode = {} if buffers is None else {"pipeline_mode": pl.Buffered(buffers)}
    return pl.BlockSpec(shape, lambda *_: (0,) * len(shape), **mode)


def cost(flops, moved):
    return pl.CostEstimate(flops=flops, bytes_accessed=moved, transcendentals=0)


def params(mib):
    return pltpu.CompilerParams(dimension_semantics=("arbitrary",), vmem_limit_bytes=mib << 20)


def start_kernel(features_ref, ids_ref, w_ref, sent_ref, held_ref, rows_ref, own_ref, sems):
    copies = [
        pltpu.make_async_copy(source, target, sems.at[i])
        for i, (source, target) in enumerate(((features_ref, rows_ref), (ids_ref, own_ref), (w_ref, held_ref)))
    ]
    for copy in copies:
        copy.start()
    copies[1].wait()
    ids = own_ref[...]
    digits = [(ids >> shift) & (255 if j == 0 else 63) for j, shift in enumerate(SHIFTS)]
    spare = jnp.zeros((ids.shape[0], LANES - len(digits) * ids.shape[1]), jnp.int32)
    codes = jnp.concatenate([*digits, spare], axis=1).astype(f32).astype(bf16)
    copies[0].wait()
    packed = jnp.concatenate([rows_ref[...], codes], axis=1)
    sent_ref[...] = jnp.broadcast_to(packed[None], sent_ref.shape)
    copies[2].wait()


def started(features, positive_ids, classifiers, times):
    rows, width = features.shape
    vmem = pl.BlockSpec(memory_space=pltpu.VMEM)
    return pl.pallas_call(
        start_kernel,
        name="start",
        out_shape=[
            jax.ShapeDtypeStruct((times, rows, width + LANES), bf16),
            jax.ShapeDtypeStruct(classifiers.shape, bf16),
        ],
        in_specs=[pl.BlockSpec(memory_space=pltpu.HBM)] * 3,
        out_specs=[vmem, vmem],
        scratch_shapes=[
            pltpu.VMEM(features.shape, features.dtype),
            pltpu.VMEM(positive_ids.shape, positive_ids.dtype),
            pltpu.SemaphoreType.DMA((3,)),
        ],
        compiler_params=pltpu.CompilerParams(vmem_limit_bytes=12 << 20),
        cost_estimate=cost(0, classifiers.size * 4),
    )(*(pltpu.with_memory_space_constraint(a, pltpu.HBM) for a in (features, positive_ids, classifiers)))


def rows_kernel(tiles_ref, rows_ref):
    rows_ref[...] = tiles_ref[...].reshape(rows_ref.shape)


def rows_of(tiles):
    count, each, width = tiles.shape
    return pl.pallas_call(
        rows_kernel,
        name="rows",
        out_shape=jax.ShapeDtypeStruct((count * each, width), tiles.dtype),
        in_specs=[pl.BlockSpec(memory_space=pltpu.VMEM)],
        out_specs=pl.BlockSpec(memory_space=pltpu.VMEM),
        compiler_params=pltpu.CompilerParams(vmem_limit_bytes=8 << 20),
        cost_estimate=cost(0, tiles.size * 4),
    )(tiles)


def sum_kernel(pieces_ref, sent_ref, *own):
    total = pieces_ref[0]
    for i in range(1, pieces_ref.shape[0]):
        total = total + pieces_ref[i]
    total = total.astype(sent_ref.dtype)
    for ref in own:
        ref[...] = total
    for i in range(sent_ref.shape[0]):
        sent_ref[i] = total


def summed(pieces, times, dtype, keep):
    one = pieces.shape[1:]
    outs = [jax.ShapeDtypeStruct((times, *one), dtype)]
    if keep:
        outs.append(jax.ShapeDtypeStruct(one, dtype))
    return pl.pallas_call(
        sum_kernel,
        name="sum_copies",
        out_shape=outs,
        in_specs=[pl.BlockSpec(memory_space=pltpu.VMEM)],
        out_specs=[pl.BlockSpec(memory_space=pltpu.VMEM)] * len(outs),
        compiler_params=pltpu.CompilerParams(vmem_limit_bytes=8 << 20),
        cost_estimate=cost(pieces.size, pieces.size * 4),
    )(pieces)


def update_kernel(ga_ref, gb_ref, ea_ref, eb_ref, w_ref, out_ref):
    change = matmul(ga_ref[...], ea_ref[...], ((0,), (0,))) + matmul(gb_ref[...], eb_ref[...], ((0,), (0,)))
    out_ref[...] = (w_ref[...].astype(f32) - learn_rate * change).astype(bf16)


def updated(grads, embs, classifiers):
    labels, width = classifiers.shape
    count = embs[0].shape[0]
    tile = LABEL_TILE
    grad_spec = pl.BlockSpec((count, tile), lambda t: (0, t))
    row_spec = pl.BlockSpec((tile, width), lambda t: (t, 0))
    return pl.pallas_call(
        update_kernel,
        name="update",
        out_shape=jax.ShapeDtypeStruct(classifiers.shape, bf16),
        grid=(labels // tile,),
        in_specs=[grad_spec, grad_spec, whole((count, width), 1), whole((count, width), 1), row_spec],
        out_specs=row_spec,
        compiler_params=params(60),
        cost_estimate=cost(4 * count * labels * width, labels * width * 4),
    )(*grads, *embs, classifiers)


def per_device(features, projection, classifiers, positive_ids):
    lab_dev, width = classifiers.shape
    rows_dev, positives = positive_ids.shape
    devices = lax.axis_size(AXES)
    total_rows = rows_dev * devices
    own = lax.axis_index(AXES)
    sent, held = started(features, positive_ids, classifiers, lax.axis_size(CHIPS))
    labels = jnp.arange(lab_dev, dtype=jnp.int32)
    lane = jnp.arange(LANES, dtype=jnp.int32)
    weight = jnp.zeros((LANES,), f32)
    for j, shift in enumerate(SHIFTS):
        weight = jnp.where(lane == own // (devices // positives) + j * positives, float(1 << shift), weight)

    base = own * lab_dev
    place = (lax.axis_index(LINE) * rows_dev).astype(jnp.uint32)
    sent, held, weight, base, place = lax.optimization_barrier((sent, held, weight, base, place))
    mine = rows_of(copies_to(sent, CHIPS))
    partner = lax.ppermute(mine, CORE, SWAP)

    def score(rows):
        emb = jnp.dot(rows[:, :width], projection, preferred_element_type=f32).astype(bf16)
        ids = jnp.sum(rows[:, width:].astype(f32) * weight[None, :], axis=1)
        label = ids.astype(jnp.int32) - base
        logits = matmul(emb, held, ((1,), (1,)))
        target = (label[:, None] == labels[None, :]).astype(f32)
        return emb, ((jax.nn.sigmoid(logits) - target) / total_rows).astype(bf16)

    emb_mine, grad_mine = score(mine)
    partner, grad_mine = lax.optimization_barrier((partner, grad_mine))
    emb_partner, grad_partner = score(partner)
    theirs = jnp.dot(grad_partner, held, preferred_element_type=f32)
    got = lax.ppermute(theirs, CORE, SWAP)
    ours = jnp.dot(grad_mine, held, preferred_element_type=f32)
    ours, got = lax.optimization_barrier((ours, got))
    ours = ours + got
    plane = lax.axis_size(PLANE)
    line = lax.axis_size(LINE)
    pieces = copies_to(ours.reshape(plane, -1, width), PLANE)
    (sent,) = summed(pieces, line, f32, False)
    sent, line_grad = summed(copies_to(sent, LINE), plane, bf16, True)
    sent, grad_mine, grad_partner = lax.optimization_barrier((sent, grad_mine, grad_partner))
    new_classifiers = updated((grad_mine, grad_partner), (emb_mine, emb_partner), classifiers)
    core_grads = copies_to(sent, PLANE).reshape(-1, width)
    core_grads, new_classifiers = lax.optimization_barrier((core_grads, new_classifiers))
    line_grad, core_grads = lax.optimization_barrier((line_grad, core_grads))
    emb_grad = lax.dynamic_slice(line_grad, (place, jnp.uint32(0)), (rows_dev, width))
    features_grad = matmul(emb_grad, projection, ((1,), (1,))).astype(bf16)
    partner_grads = lax.ppermute(core_grads, CORE, SWAP)
    first = matmul(mine[:, :width], core_grads, ((0,), (0,)))
    first, partner_grads, features_grad = lax.optimization_barrier((first, partner_grads, features_grad))
    projection_grad = (first + matmul(partner[:, :width], partner_grads, ((0,), (0,)))).astype(bf16)
    return new_classifiers, projection_grad, features_grad


def solution(mesh):
    torus = Mesh(mesh.devices.reshape(4, 2, 2, 4, 4), AXES)
    placed = (P(AXES, None), P(), P(AXES, None), P(AXES, None))
    return jax.shard_map(
        per_device,
        mesh=torus,
        in_specs=placed,
        out_specs=(P(AXES, None), P(), P(AXES, None)),
        check_vma=False,
    )
```

```python
import jax
import jax.numpy as jnp
from jax import lax
from jax.experimental import pallas as pl
from jax.experimental.pallas import tpu as pltpu
from jax.sharding import Mesh
from jax.sharding import PartitionSpec as P

AXES = ("zl", "core", "zh", "y", "x")
PLANE = ("y", "x")
LINE = ("zh", "zl")
CHIPS = PLANE + LINE
CORE = "core"
SWAP = ((0, 1), (1, 0))
LANES = 128
SHIFTS = (12, 6, 0)
UPDATE_TILE = 768

learn_rate = 1.0
bf16 = jnp.bfloat16
f32 = jnp.float32


def copies_to(sent, axes):
    return lax.all_to_all(sent, axes, 0, 0, tiled=True)


def matmul(a, b, over):
    return lax.dot_general(a, b, (over, ((), ())), preferred_element_type=f32)


def whole(shape, buffers=None):
    mode = {} if buffers is None else {"pipeline_mode": pl.Buffered(buffers)}
    return pl.BlockSpec(shape, lambda *_: (0,) * len(shape), **mode)


def cost(flops, moved):
    return pl.CostEstimate(flops=flops, bytes_accessed=moved, transcendentals=0)


def params(mib):
    return pltpu.CompilerParams(dimension_semantics=("arbitrary",), vmem_limit_bytes=mib << 20)


def start_kernel(features_ref, ids_ref, w_ref, sent_ref, held_ref, rows_ref, own_ref, sems):
    copies = [
        pltpu.make_async_copy(source, target, sems.at[i])
        for i, (source, target) in enumerate(((features_ref, rows_ref), (ids_ref, own_ref), (w_ref, held_ref)))
    ]
    for copy in copies:
        copy.start()
    copies[1].wait()
    ids = own_ref[...]
    digits = [(ids >> shift) & (255 if j == 0 else 63) for j, shift in enumerate(SHIFTS)]
    spare = jnp.zeros((ids.shape[0], LANES - len(digits) * ids.shape[1]), jnp.int32)
    codes = jnp.concatenate([*digits, spare], axis=1).astype(f32).astype(bf16)
    copies[0].wait()
    packed = jnp.concatenate([rows_ref[...], codes], axis=1)
    sent_ref[...] = jnp.broadcast_to(packed[None], sent_ref.shape)
    copies[2].wait()


def started(features, positive_ids, projection, times):
    rows, width = features.shape
    vmem = pl.BlockSpec(memory_space=pltpu.VMEM)
    return pl.pallas_call(
        start_kernel,
        name="start",
        out_shape=[
            jax.ShapeDtypeStruct((times, rows, width + LANES), bf16),
            jax.ShapeDtypeStruct(projection.shape, bf16),
        ],
        in_specs=[pl.BlockSpec(memory_space=pltpu.HBM)] * 3,
        out_specs=[vmem, vmem],
        scratch_shapes=[
            pltpu.VMEM(features.shape, features.dtype),
            pltpu.VMEM(positive_ids.shape, positive_ids.dtype),
            pltpu.SemaphoreType.DMA((3,)),
        ],
        compiler_params=pltpu.CompilerParams(vmem_limit_bytes=12 << 20),
        cost_estimate=cost(0, projection.size * 4),
    )(*(pltpu.with_memory_space_constraint(a, pltpu.HBM) for a in (features, positive_ids, projection)))


def rows_kernel(tiles_ref, rows_ref):
    rows_ref[...] = tiles_ref[...].reshape(rows_ref.shape)


def rows_of(tiles):
    count, each, width = tiles.shape
    return pl.pallas_call(
        rows_kernel,
        name="rows",
        out_shape=jax.ShapeDtypeStruct((count * each, width), tiles.dtype),
        in_specs=[pl.BlockSpec(memory_space=pltpu.VMEM)],
        out_specs=pl.BlockSpec(memory_space=pltpu.VMEM),
        compiler_params=pltpu.CompilerParams(vmem_limit_bytes=8 << 20),
        cost_estimate=cost(0, tiles.size * 4),
    )(tiles)


def sum_kernel(pieces_ref, sent_ref, *own):
    total = pieces_ref[0]
    for i in range(1, pieces_ref.shape[0]):
        total = total + pieces_ref[i]
    total = total.astype(sent_ref.dtype)
    for ref in own:
        ref[...] = total
    for i in range(sent_ref.shape[0]):
        sent_ref[i] = total


def summed(pieces, times, dtype, keep):
    one = pieces.shape[1:]
    outs = [jax.ShapeDtypeStruct((times, *one), dtype)]
    if keep:
        outs.append(jax.ShapeDtypeStruct(one, dtype))
    return pl.pallas_call(
        sum_kernel,
        name="sum_copies",
        out_shape=outs,
        in_specs=[pl.BlockSpec(memory_space=pltpu.VMEM)],
        out_specs=[pl.BlockSpec(memory_space=pltpu.VMEM)] * len(outs),
        compiler_params=pltpu.CompilerParams(vmem_limit_bytes=8 << 20),
        cost_estimate=cost(pieces.size, pieces.size * 4),
    )(pieces)


def line_kernel(shifts, at_ref, own_ref, *refs):
    moved, out_ref = refs[:-1], refs[-1]
    count = len(shifts) + 1
    total = None
    for source in range(count):
        back = lax.rem(at_ref[0] - source + count, count)
        value = own_ref[...]
        for shift, ref in zip(shifts, moved):
            value = jnp.where(back == shift, ref[...], value)
        total = value if total is None else total + value
    out_ref[...] = total


def line_summed(at, own, moved, shifts):
    vmem = pl.BlockSpec(memory_space=pltpu.VMEM)

    def body(*refs):
        line_kernel(shifts, *refs)

    return pl.pallas_call(
        body,
        name="line_sum",
        out_shape=jax.ShapeDtypeStruct(own.shape, own.dtype),
        in_specs=[pl.BlockSpec(memory_space=pltpu.SMEM)] + [vmem] * (1 + len(moved)),
        out_specs=vmem,
        compiler_params=pltpu.CompilerParams(vmem_limit_bytes=8 << 20),
        cost_estimate=cost(own.size * 4, own.size * 20),
    )(at, own, *moved)


def pair_kernel(near_ref, far_ref, sent_ref, own_ref):
    total = (near_ref[...] + far_ref[...]).astype(bf16)
    own_ref[...] = total
    for i in range(sent_ref.shape[0]):
        sent_ref[i] = total


def paired(near, far, times):
    vmem = pl.BlockSpec(memory_space=pltpu.VMEM)
    return pl.pallas_call(
        pair_kernel,
        name="pair_copies",
        out_shape=[jax.ShapeDtypeStruct((times, *near.shape), bf16), jax.ShapeDtypeStruct(near.shape, bf16)],
        in_specs=[vmem, vmem],
        out_specs=[vmem, vmem],
        compiler_params=pltpu.CompilerParams(vmem_limit_bytes=8 << 20),
        cost_estimate=cost(near.size, near.size * 8),
    )(near, far)


def update_kernel(ga_ref, gb_ref, ea_ref, eb_ref, w_ref, out_ref, fresh_ref, sems):
    tile = UPDATE_TILE
    copies = []
    for i in range(w_ref.shape[0] // tile):
        cut = slice(i * tile, (i + 1) * tile)
        change = matmul(ga_ref[:, cut], ea_ref[...], ((0,), (0,))) + matmul(gb_ref[:, cut], eb_ref[...], ((0,), (0,)))
        fresh_ref[cut, :] = (w_ref[cut, :].astype(f32) - learn_rate * change).astype(bf16)
        there = pl.ds(i * tile, tile)
        copies.append(pltpu.make_async_copy(fresh_ref.at[there], out_ref.at[there], sems.at[i]))
        copies[-1].start()
    for copy in copies:
        copy.wait()


def updated(grads, embs, held):
    labels, width = held.shape
    count = embs[0].shape[0]
    return pl.pallas_call(
        update_kernel,
        name="update",
        out_shape=jax.ShapeDtypeStruct(held.shape, bf16),
        in_specs=[pl.BlockSpec(memory_space=pltpu.VMEM)] * 5,
        out_specs=pl.BlockSpec(memory_space=pltpu.HBM),
        scratch_shapes=[pltpu.VMEM(held.shape, bf16), pltpu.SemaphoreType.DMA((labels // UPDATE_TILE,))],
        compiler_params=pltpu.CompilerParams(vmem_limit_bytes=16 << 20),
        cost_estimate=cost(4 * count * labels * width, labels * width * 2),
    )(*grads, *embs, held)


def per_device(features, projection, classifiers, positive_ids):
    lab_dev, width = classifiers.shape
    rows_dev, positives = positive_ids.shape
    devices = lax.axis_size(AXES)
    total_rows = rows_dev * devices
    own = lax.axis_index(AXES)
    sent, projection = started(features, positive_ids, projection, lax.axis_size(CHIPS))
    held = classifiers
    labels = jnp.arange(lab_dev, dtype=jnp.int32)
    lane = jnp.arange(LANES, dtype=jnp.int32)
    weight = jnp.zeros((LANES,), f32)
    for j, shift in enumerate(SHIFTS):
        weight = jnp.where(lane == own // (devices // positives) + j * positives, float(1 << shift), weight)

    base = own * lab_dev
    place = (lax.axis_index(LINE) * rows_dev).astype(jnp.uint32)
    at_z = lax.axis_index("zl").reshape(1)
    sent, projection, weight, base, place, at_z = lax.optimization_barrier((sent, projection, weight, base, place, at_z))
    mine = rows_of(copies_to(sent, CHIPS))
    partner = lax.ppermute(mine, CORE, SWAP)

    def score(rows):
        emb = jnp.dot(rows[:, :width], projection, preferred_element_type=f32).astype(bf16)
        ids = jnp.sum(rows[:, width:].astype(f32) * weight[None, :], axis=1)
        label = ids.astype(jnp.int32) - base
        logits = matmul(emb, held, ((1,), (1,)))
        target = (label[:, None] == labels[None, :]).astype(f32)
        return emb, ((jax.nn.sigmoid(logits) - target) / total_rows).astype(bf16)

    emb_mine, grad_mine = score(mine)
    partner, grad_mine = lax.optimization_barrier((partner, grad_mine))
    emb_partner, grad_partner = score(partner)
    theirs = jnp.dot(grad_partner, held, preferred_element_type=f32)
    got = lax.ppermute(theirs, CORE, SWAP)
    ours = jnp.dot(grad_mine, held, preferred_element_type=f32)
    ours, got = lax.optimization_barrier((ours, got))
    ours = ours + got
    plane = lax.axis_size(PLANE)
    pieces = copies_to(ours.reshape(plane, -1, width), PLANE)
    (near,) = summed(pieces, 1, f32, False)
    near = near[0]
    count = lax.axis_size("zl")
    shifts = (2, 1, 3)
    moved = [lax.ppermute(near, "zl", tuple((i, (i + k) % count) for i in range(count))) for k in shifts]
    near, grad_mine, grad_partner = lax.optimization_barrier((near, grad_mine, grad_partner))
    new_classifiers = updated((grad_mine, grad_partner), (emb_mine, emb_partner), held)
    near, new_classifiers, *moved = lax.optimization_barrier((near, new_classifiers, *moved))
    near = line_summed(at_z, near, moved, shifts)
    far = lax.ppermute(near, "zh", SWAP)
    sent, line_grad = paired(near, far, plane)
    core_grads = copies_to(sent, PLANE).reshape(-1, width)
    line_grad, core_grads = lax.optimization_barrier((line_grad, core_grads))
    emb_grad = lax.dynamic_slice(line_grad, (place, jnp.uint32(0)), (rows_dev, width))
    features_grad = matmul(emb_grad, projection, ((1,), (1,))).astype(bf16)
    partner_grads = lax.ppermute(core_grads, CORE, SWAP)
    first = matmul(mine[:, :width], core_grads, ((0,), (0,)))
    first, partner_grads, features_grad = lax.optimization_barrier((first, partner_grads, features_grad))
    projection_grad = (first + matmul(partner[:, :width], partner_grads, ((0,), (0,)))).astype(bf16)
    return new_classifiers, projection_grad, features_grad


def solution(mesh):
    torus = Mesh(mesh.devices.reshape(4, 2, 2, 4, 4), AXES)
    placed = (P(AXES, None), P(), P(AXES, None), P(AXES, None))
    return jax.shard_map(
        per_device,
        mesh=torus,
        in_specs=placed,
        out_specs=(P(AXES, None), P(), P(AXES, None)),
        check_vma=False,
    )
```
